32 devices in a mesh: row: 8 (over y, x, core), col: 4 (over z).
Axes of the slice: x: 2, y: 2, z: 4, core: 2. Of those that a mesh axis runs over, the one named last changes fastest.
Arguments:
- latents: bfloat16 [256, 64, 1024], P('row', 'col'), may hold values from -6 to 6
- row_qkv: bfloat16 [1024, 3072], replicated, may hold values from -2 to 2, as said below
- row_out: bfloat16 [1024, 1024], replicated, may hold values from -0.75 to 0.75
- col_qkv: bfloat16 [1024, 3072], replicated, may hold values from -2 to 2, as said below
- col_out: bfloat16 [1024, 1024], replicated, may hold values from -0.75 to 0.75
- up_weight: bfloat16 [1024, 2048], replicated, may hold values from -0.1875 to 0.1875
- down_weight: bfloat16 [2048, 1024], replicated, may hold values from -0.25 to 0.25
Outputs:
- result: bfloat16 [256, 64, 1024], P('row', 'col')
The draws below stay inside these ranges and needn't reach their ends.
Inputs may be any that keep to these rules, and one draw needn't show every extreme that they name: `row_qkv`: a projection matrix. `col_qkv`: a projection matrix.
All inputs are finite; a program needn't handle non-finite values.
Results may differ from the reference program's by a relative error of at most 0.02.
Values may be sent and summed in bfloat16 or wider, within the bound.
No kernel may reach another device: no remote copies, remote signals or barrier semaphores. Data moves between devices by JAX's collectives and lax.ppermute only.
A program may use at most 192 MiB of HBM per device.

```python
import math
import jax
import jax.numpy as jnp
from jax import lax

D = 1024
HEADS = 8
FF = 2048
GH = 256
GW = 64


def make_projection(key):
    base = jax.random.normal(key, (D, 3 * D), jnp.float32) / math.sqrt(D)
    base = jnp.clip(base, -3.0 / math.sqrt(D) * 2.0, 3.0 / math.sqrt(D) * 2.0)
    return base


def draw_row_qkv(key, part):
    return make_projection(jax.random.fold_in(key, 11)).astype(jnp.bfloat16)


def draw_col_qkv(key, part):
    return make_projection(jax.random.fold_in(key, 23)).astype(jnp.bfloat16)


def steps_of(rng, dims, cuts, low, high):
    def one(dim, shards_of):
        steps = jax.random.uniform(jax.random.fold_in(jax.random.fold_in(rng, 6), dim), (shards_of,), jnp.float32, low / len(cuts), high / len(cuts))
        return jnp.repeat(jnp.exp(steps), dims[dim] // shards_of).reshape((-1,) + (1,) * (len(dims) - dim - 1))

    gain = one(*cuts[0])
    for cut in cuts[1:]:
        gain = gain * one(*cut)
    return gain


def normal_values(key, dims, spread, bound, shards=(), kind=jnp.bfloat16):
    drawn = spread * jax.random.normal(key, dims, jnp.float32)
    if shards:
        drawn = drawn * steps_of(key, dims, shards, -0.22, 0.18)
    return jnp.clip(drawn, -bound, bound).astype(kind)


def setup_inputs(seed: int = 0) -> dict:
    arg_keys = jax.random.split(jax.random.key(seed), 8)
    latents = normal_values(arg_keys[0], (GH, GW, D), 1.0, 6.0, ((0, 8), (1, 4)))
    row_qkv = draw_row_qkv(jax.random.fold_in(arg_keys[7], 71), 0)
    row_out = normal_values(arg_keys[2], (D, D), (D // 16) ** -0.5, 0.75)
    col_qkv = draw_col_qkv(jax.random.fold_in(arg_keys[7], 71), 0)
    col_out = normal_values(arg_keys[4], (D, D), (D // 16) ** -0.5, 0.75)
    up_weight = normal_values(arg_keys[5], (D, FF), D ** -0.5, 0.1875)
    down_weight = normal_values(arg_keys[6], (FF, D), (FF // 4) ** -0.5, 0.25)
    return {"latents": latents, "row_qkv": row_qkv, "row_out": row_out, "col_qkv": col_qkv, "col_out": col_out, "up_weight": up_weight, "down_weight": down_weight}


def normalize(values):
    wide = values.astype(jnp.float32)
    return (wide * lax.rsqrt(lax.optimization_barrier(jnp.mean(wide * wide, -1, keepdims=True)) + 1e-06)).astype(jnp.bfloat16)

def project(normed, weight):
    rows, cols = (normed.shape[0], normed.shape[1])
    flat = jnp.dot(normed.reshape(rows * cols, D), weight, preferred_element_type=jnp.float32)
    return flat.astype(jnp.bfloat16).reshape(rows, cols, 3, HEADS, D // HEADS)

def attend_rows(query, keys, values):
    scale = 1.0 / (D // HEADS) ** 0.5
    scores = jnp.einsum('aqhd,akhd->ahqk', query.astype(jnp.float32), keys.astype(jnp.float32), precision=lax.Precision.HIGHEST) * scale
    probs = jax.nn.softmax(scores, -1).astype(jnp.bfloat16)
    return jnp.einsum('ahqk,akhd->aqhd', probs.astype(jnp.float32), values.astype(jnp.float32), precision=lax.Precision.HIGHEST).astype(jnp.bfloat16)

def attend_cols(query, keys, values):
    scale = 1.0 / (D // HEADS) ** 0.5
    scores = jnp.einsum('qbhd,kbhd->bhqk', query.astype(jnp.float32), keys.astype(jnp.float32), precision=lax.Precision.HIGHEST) * scale
    probs = jax.nn.softmax(scores, -1).astype(jnp.bfloat16)
    return jnp.einsum('bhqk,kbhd->qbhd', probs.astype(jnp.float32), values.astype(jnp.float32), precision=lax.Precision.HIGHEST).astype(jnp.bfloat16)

def add_projected(base, mixed, weight):
    rows, cols = (base.shape[0], base.shape[1])
    term = jnp.dot(mixed.reshape(rows * cols, D), weight, preferred_element_type=jnp.float32).reshape(rows, cols, D)
    return (base.astype(jnp.float32) + term).astype(jnp.bfloat16)

def reference(latents, row_qkv, row_out, col_qkv, col_out, up_weight, down_weight):
    rows, cols = (latents.shape[0], latents.shape[1])
    proj1 = project(normalize(latents), row_qkv)
    mixed1 = attend_rows(proj1[:, :, 0], proj1[:, :, 1], proj1[:, :, 2])
    after1 = add_projected(latents, mixed1, row_out)
    proj2 = project(normalize(after1), col_qkv)
    mixed2 = attend_cols(proj2[:, :, 0], proj2[:, :, 1], proj2[:, :, 2])
    after2 = add_projected(after1, mixed2, col_out)
    normed3 = normalize(after2).reshape(rows * cols, D)
    hidden = jax.nn.gelu(jnp.dot(normed3, up_weight, preferred_element_type=jnp.float32), approximate=True).astype(jnp.bfloat16)
    term = jnp.dot(hidden, down_weight, preferred_element_type=jnp.float32).reshape(rows, cols, D)
    return (after2.astype(jnp.float32) + term).astype(jnp.bfloat16)
```

```python
import functools
import math

import jax
import jax.numpy as jnp
from jax import lax
from jax.experimental import pallas as pl
from jax.experimental.pallas import tpu as pltpu
from jax.sharding import PartitionSpec as P

HEADS = 8
PAIR = 2
CHUNKS = 2
BF = jnp.bfloat16
F32 = jnp.float32


def normalize(wide):
    return (wide * lax.rsqrt(jnp.mean(wide * wide, -1, keepdims=True) + 1e-06)).astype(BF)


def dot(a, b):
    return jnp.dot(a, b, preferred_element_type=F32)


def dot_t(a, b):
    return lax.dot_general(a, b, (((1,), (1,)), ((), ())), preferred_element_type=F32)


def attend(q, k, v, mask):
    gain = math.log2(math.e) / math.sqrt(q.shape[-1])
    s = dot_t(q, k)
    if mask is not None:
        s = jnp.where(mask, s, -1e30)
    e = jnp.exp2((s - jnp.max(s, -1, keepdims=True)) * gain).astype(BF)
    both = dot(e, jnp.concatenate([v, jnp.ones_like(v)], -1))
    width = v.shape[-1]
    return (both[:, :width] / both[:, width:]).astype(BF)


def one_hot(source, size):
    return (lax.broadcasted_iota(jnp.int32, (source.shape[0], size), 1) == source).astype(BF)


def row_kernel(g, idx_ref, *refs):
    nc, nr, rows, cols, cpd = g["nc"], g["nr"], g["rows"], g["cols"], g["cpd"]
    xs, (wq, wk, wv, wo), outs = refs[:nc], refs[nc : nc + 4], refs[nc + 4 : 2 * nc + 4]
    normed, acc = refs[2 * nc + 4 :]
    tokens, line = rows * nc * cols, nc * cols
    step = pl.program_id(0)

    def load():
        parts = [xs[k][i * cols : (i + 1) * cols, :] for i in range(rows) for k in range(nc)]
        return jnp.concatenate(parts, 0).astype(F32)

    @pl.when(step == 0)
    def _():
        normed[...] = normalize(load())
        acc[...] = jnp.zeros_like(acc)

    n = normed[...]
    q, k, v = dot(n, wq[...]).astype(BF), dot(n, wk[...]).astype(BF), dot(n, wv[...]).astype(BF)
    width = q.shape[-1] // PAIR
    group = min(max(line, 128), tokens)
    mask = None
    if group > line:
        a = lax.broadcasted_iota(jnp.int32, (group, group), 0) // line
        b = lax.broadcasted_iota(jnp.int32, (group, group), 1) // line
        mask = a == b
    heads = []
    for h in range(PAIR):
        lanes = slice(h * width, (h + 1) * width)
        parts = []
        for t in range(0, tokens, group):
            span = slice(t, t + group)
            parts.append(attend(q[span, lanes], k[span, lanes], v[span, lanes], mask))
        heads.append(jnp.concatenate(parts, 0))
    acc[...] += dot(jnp.concatenate(heads, -1), wo[...])

    @pl.when(step == pl.num_programs(0) - 1)
    def _():
        after = (load() + acc[...]).astype(BF)
        o = lax.broadcasted_iota(jnp.int32, (tokens, 1), 0)
        i, jj, m, k = o % rows, (o // rows) % cpd, (o // (rows * cpd)) % nr, o // (rows * cols)
        source = (i * nc + k) * cols + cpd * jnp.bitwise_xor(m, idx_ref[0]) + jj
        moved = dot(one_hot(source, tokens), after).astype(BF)
        for k in range(nc):
            outs[k][...] = moved[k * rows * cols : (k + 1) * rows * cols, :]


def row_stage(g, idx, slots, row_qkv, row_out):
    nc, tokens = g["nc"], g["rows"] * g["nc"] * g["cols"]
    width = row_out.shape[0]
    block = width * PAIR // HEADS
    steps = HEADS // PAIR
    part = tokens // nc
    whole = pl.BlockSpec((part, width), lambda p: (0, 0))
    third = [pl.BlockSpec((width, block), functools.partial(lambda t, p: (0, t * steps + p), t)) for t in range(3)]
    return pl.pallas_call(
        functools.partial(row_kernel, g),
        grid=(steps,),
        in_specs=[pl.BlockSpec(memory_space=pltpu.SMEM)] + [whole] * nc + third + [pl.BlockSpec((block, width), lambda p: (p, 0))],
        out_specs=[whole] * nc,
        out_shape=[jax.ShapeDtypeStruct((part, width), BF)] * nc,
        scratch_shapes=[pltpu.VMEM((tokens, width), BF), pltpu.VMEM((tokens, width), F32)],
        cost_estimate=pl.CostEstimate(flops=8 * tokens * width * width, bytes_accessed=8 * width * width + 4 * tokens * width, transcendentals=0),
        name="row_stage",
    )(idx, *slots, row_qkv, row_qkv, row_qkv, row_out)


def project_kernel(g, *refs):
    nr, part, cpd, rows = g["nr"], g["part"], g["cpd"], g["rows"]
    xs, (wq, wk, wv), (q, k, v, x_out), (normed,) = refs[:nr], refs[nr : nr + 3], refs[nr + 3 : nr + 7], refs[nr + 7 :]

    @pl.when(pl.program_id(0) == 0)
    def _():
        x = gather_columns(g, xs)
        x_out[...] = x.astype(BF)
        normed[...] = normalize(x)

    n = normed[...]
    q[...], k[...], v[...] = dot(n, wq[...]).astype(BF), dot(n, wk[...]).astype(BF), dot(n, wv[...]).astype(BF)


def gather_columns(g, xs):
    cpd, rows = g["cpd"], g["rows"]
    x = jnp.concatenate([ref[...] for ref in xs], 0)
    tokens = x.shape[0]
    o = lax.broadcasted_iota(jnp.int32, (tokens, 1), 0)
    per = tokens // cpd
    jj, mk, i = o // per, (o % per) // rows, o % rows
    return dot(one_hot((mk * cpd + jj) * rows + i, tokens), x)


def project_stage(g, slots, col_qkv):
    nr, part = g["nr"], g["part"]
    width = col_qkv.shape[0]
    tokens = nr * part
    steps = HEADS // PAIR
    block = width // steps
    whole = pl.BlockSpec((part, width), lambda p: (0, 0))
    third = [pl.BlockSpec((width, block), functools.partial(lambda t, p: (0, t * steps + p), t)) for t in range(3)]
    out = jax.ShapeDtypeStruct((tokens, width), BF)
    return pl.pallas_call(
        functools.partial(project_kernel, g),
        grid=(steps,),
        in_specs=[whole] * nr + third,
        out_specs=[pl.BlockSpec((tokens, block), lambda p: (0, p))] * 3 + [pl.BlockSpec((tokens, width), lambda p: (0, 0))],
        out_shape=[out] * 4,
        scratch_shapes=[pltpu.VMEM((tokens, width), BF)],
        cost_estimate=pl.CostEstimate(flops=6 * tokens * width * width, bytes_accessed=6 * width * width + 12 * tokens * width, transcendentals=0),
        name="project_stage",
    )(*slots, col_qkv, col_qkv, col_qkv)


def col_kernel(g, *refs):
    nr, cpd, half = g["nr"], g["cpd"], g["half"]
    n_old = 4 * (CHUNKS - 1)
    xs, old = refs[:nr], refs[nr : nr + n_old]
    wq, wk, wv, wo = refs[nr + n_old : nr + n_old + 4]
    outs = refs[nr + n_old + 4 : nr + n_old + 6]
    x_new, normed, acc = refs[nr + n_old + 6 :]
    step = pl.program_id(0)

    @pl.when(step == 0)
    def _():
        x = gather_columns(g, xs)
        x_new[...] = x.astype(BF)
        normed[...] = normalize(x)
        acc[...] = jnp.zeros_like(acc)

    n = normed[...]
    new = [dot(n, w[...]).astype(BF) for w in (wq, wk, wv)]
    per = n.shape[0] // cpd
    width = new[0].shape[-1] // PAIR

    def column(which, jj):
        span = slice(jj * per, (jj + 1) * per)
        return jnp.concatenate([old[4 * t + which][span, :] for t in range(CHUNKS - 1)] + [new[which][span, :]], 0)

    columns = []
    for jj in range(cpd):
        q, k, v = (column(which, jj) for which in range(3))
        heads = [attend(*(a[:, h * width : (h + 1) * width] for a in (q, k, v)), None) for h in range(PAIR)]
        columns.append(jnp.concatenate(heads, -1))
    acc[...] += dot(jnp.concatenate(columns, 0), wo[...])

    @pl.when(step == pl.num_programs(0) - 1)
    def _():
        each = per // nr
        for jj in range(cpd):
            for t in range(CHUNKS):
                src = x_new if t == CHUNKS - 1 else old[4 * t + 3]
                base = (jj * CHUNKS + t) * per
                after = (src[jj * per : (jj + 1) * per, :].astype(F32) + acc[base : base + per, :]).astype(BF)
                at = (jj * CHUNKS + t) * half * each
                outs[0][at : at + half * each, :] = after[: half * each, :]
                outs[1][at : at + half * each, :] = after[half * each :, :]


def col_stage(g, slots, old, col_qkv, col_out):
    nr, part = g["nr"], g["part"]
    width = col_qkv.shape[0]
    tokens = nr * part
    total = tokens * CHUNKS
    steps = HEADS // PAIR
    block = width // steps
    whole = pl.BlockSpec((part, width), lambda p: (0, 0))
    third = [pl.BlockSpec((width, block), functools.partial(lambda t, p: (0, t * steps + p), t)) for t in range(3)]
    one = [pl.BlockSpec((tokens, block), lambda p: (0, p))] * 3 + [pl.BlockSpec((tokens, width), lambda p: (0, 0))]
    return pl.pallas_call(
        functools.partial(col_kernel, g),
        grid=(steps,),
        in_specs=[whole] * nr + one * (CHUNKS - 1) + third + [pl.BlockSpec((block, width), lambda p: (p, 0))],
        out_specs=[pl.BlockSpec((total // 2, width), lambda p: (0, 0))] * 2,
        out_shape=[jax.ShapeDtypeStruct((total // 2, width), BF)] * 2,
        scratch_shapes=[pltpu.VMEM((tokens, width), BF), pltpu.VMEM((tokens, width), BF), pltpu.VMEM((total, width), F32)],
        cost_estimate=pl.CostEstimate(flops=8 * tokens * width * width + 4 * total * total * width // cpd_of(g), bytes_accessed=8 * width * width + 10 * total * width, transcendentals=0),
        name="col_stage",
    )(*slots, *old, col_qkv, col_qkv, col_qkv, col_out)


def cpd_of(g):
    return g["cpd"]


def ffn_kernel(g, idx_ref, x_ref, up, down, *refs):
    half, nc, rows, cpd = g["half"], g["nc"], g["rows"], g["cpd"]
    outs, (normed, acc) = refs[:half], refs[half:]
    step = pl.program_id(0)

    @pl.when(step == 0)
    def _():
        normed[...] = normalize(x_ref[...].astype(F32))
        acc[...] = jnp.zeros_like(acc)

    hidden = jax.nn.gelu(dot(normed[...], up[...]), approximate=True).astype(BF)
    acc[...] += dot(hidden, down[...])

    @pl.when(step == pl.num_programs(0) - 1)
    def _():
        result = (x_ref[...].astype(F32) + acc[...]).astype(BF)
        tokens = result.shape[0]
        o = lax.broadcasted_iota(jnp.int32, (tokens, 1), 0)
        jj, i, t = o % cpd, (o // cpd) % rows, (o // (cpd * rows)) % CHUNKS
        c, m = (o // (cpd * rows * CHUNKS)) % nc, o // (cpd * rows * CHUNKS * nc)
        k = jnp.bitwise_xor(c, idx_ref[1])
        source = (((jj * CHUNKS + t) * half + m) * nc + k) * rows + i
        moved = dot(one_hot(source, tokens), result).astype(BF)
        each = tokens // half
        for m in range(half):
            outs[m][...] = moved[m * each : (m + 1) * each, :]


def ffn_stage(g, idx, x, up_weight, down_weight):
    tokens, width = x.shape
    hidden = up_weight.shape[1]
    block = min(512, hidden)
    half = g["half"]
    each = tokens // half
    whole = pl.BlockSpec((tokens, width), lambda p: (0, 0))
    return pl.pallas_call(
        functools.partial(ffn_kernel, g),
        grid=(hidden // block,),
        in_specs=[pl.BlockSpec(memory_space=pltpu.SMEM), whole, pl.BlockSpec((width, block), lambda p: (0, p)), pl.BlockSpec((block, width), lambda p: (p, 0))],
        out_specs=[pl.BlockSpec((each, width), lambda p: (0, 0))] * half,
        out_shape=[jax.ShapeDtypeStruct((each, width), BF)] * half,
        scratch_shapes=[pltpu.VMEM((tokens, width), BF), pltpu.VMEM((tokens, width), F32)],
        cost_estimate=pl.CostEstimate(flops=4 * tokens * width * hidden, bytes_accessed=4 * width * hidden + 4 * tokens * width, transcendentals=0),
        name="ffn_stage",
    )(idx, x, up_weight, down_weight)


def final_kernel(g, idx_ref, *refs):
    nr, cpd, cols, span = g["nr"], g["cpd"], g["cols"], g["span"]
    ins, out = refs[:nr], refs[nr]
    tokens = span * cols
    o = lax.broadcasted_iota(jnp.int32, (tokens, 1), 0)
    w, j = o // cols, o % cols
    m = jnp.bitwise_xor(j // cpd, idx_ref[0])
    pick = one_hot((m * span + w) * cpd + j % cpd, tokens)
    rows = ins[0].shape[0] // cpd
    for a in range(0, rows, span):
        x = jnp.concatenate([ref[a * cpd : (a + span) * cpd, :] for ref in ins], 0)
        out[a * cols : (a + span) * cols, :] = dot(pick, x).astype(BF)


def final_stage(g, idx, slots):
    nr = g["nr"]
    each, width = slots[0].shape
    total = nr * each
    return pl.pallas_call(
        functools.partial(final_kernel, g),
        in_specs=[pl.BlockSpec(memory_space=pltpu.SMEM)] + [pl.BlockSpec(memory_space=pltpu.VMEM)] * nr,
        out_specs=pl.BlockSpec(memory_space=pltpu.VMEM),
        out_shape=jax.ShapeDtypeStruct((total, width), BF),
        cost_estimate=pl.CostEstimate(flops=2 * total * width * g["span"] * g["cols"], bytes_accessed=4 * total * width, transcendentals=0),
        name="final_stage",
    )(idx, *slots)


def swap(x, axis, size, k):
    return x if k == 0 else lax.ppermute(x, axis, [(i, i ^ k) for i in range(size)])


def on_device(nr, nc, latents, row_qkv, row_out, col_qkv, col_out, up_weight, down_weight):
    local_rows, cols, width = latents.shape
    band = local_rows // nc
    rows = band // CHUNKS
    cpd = cols // nr
    g = dict(nr=nr, nc=nc, rows=rows, cols=cols, cpd=cpd, part=nc * rows * cpd, half=nr // 2, span=8)
    r, c = lax.axis_index("row"), lax.axis_index("col")
    idx = jnp.stack([r, c]).astype(jnp.int32)

    inbound = []
    for t in range(CHUNKS):
        slots = []
        for k in range(nc):
            at = jnp.bitwise_xor(c, k) * band + t * rows
            piece = lax.dynamic_slice_in_dim(latents, at, rows, 0).reshape(rows * cols, width)
            slots.append(piece)
        order = sorted(range(1, nc), key=lambda k: -k)
        got = {k: swap(slots[k], "col", nc, k) for k in order}
        inbound.append([slots[0]] + [got[k] for k in range(1, nc)])

    arrived = []
    for t in range(CHUNKS):
        outs = row_stage(g, idx, inbound[t], row_qkv, row_out)
        order = sorted(range(1, nc), key=lambda k: -k)
        back = {k: swap(outs[k], "col", nc, k) for k in order}
        back[0] = outs[0]
        size = rows * cpd
        sends = [jnp.concatenate([back[k][m * size : (m + 1) * size] for k in range(nc)], 0) for m in range(nr)]
        arrived.append([swap(sends[m], "row", nr, m) for m in range(nr)])

    old = []
    for t in range(CHUNKS - 1):
        old += project_stage(g, arrived[t], col_qkv)
    halves = col_stage(g, arrived[-1], old, col_qkv, col_out)
    final = [None] * nr
    for b in (1, 0):
        outs = ffn_stage(g, idx, halves[b], up_weight, down_weight)
        for m in range(g["half"]):
            slot = b * g["half"] + m
            final[slot] = swap(outs[m], "row", nr, slot)
    return final_stage(g, idx, final).reshape(local_rows, cols, width)


def solution(mesh):
    in_specs = (P("row", "col", None), P(), P(), P(), P(), P(), P())
    return jax.shard_map(
        functools.partial(on_device, mesh.shape["row"], mesh.shape["col"]),
        mesh=mesh,
        in_specs=in_specs,
        out_specs=P("row", "col", None),
        check_vma=False,
    )
```

```python
import functools
import math

import jax
import jax.numpy as jnp
from jax import lax
from jax.experimental import pallas as pl
from jax.experimental.pallas import tpu as pltpu
from jax.sharding import PartitionSpec as P


HEADS = 8
CHUNKS = 2
BF = jnp.bfloat16
F32 = jnp.float32


def normalize(wide):
    return (wide * lax.rsqrt(jnp.mean(wide * wide, -1, keepdims=True) + 1e-06)).astype(BF)


def dot(a, b):
    return jnp.dot(a, b, preferred_element_type=F32)


def dot_t(a, b):
    return lax.dot_general(a, b, (((1,), (1,)), ((), ())), preferred_element_type=F32)


def attend(units, mask):
    scores = [dot_t(q, k) for q, k, _ in units]
    weights = []
    for s, (q, _, _) in zip(scores, units):
        gain = math.log2(math.e) / math.sqrt(q.shape[-1])
        if mask is not None:
            s = jnp.where(mask, s, -1e30)
        weights.append(jnp.exp2((s - jnp.max(s, -1, keepdims=True)) * gain).astype(BF))
    outs = []
    for e, (_, _, v) in zip(weights, units):
        both = dot(e, jnp.concatenate([v, jnp.ones_like(v)], -1))
        width = v.shape[-1]
        outs.append((both[:, :width] / both[:, width:]).astype(BF))
    return outs


def one_hot(source, size):
    return (lax.broadcasted_iota(jnp.int32, (source.shape[0], size), 1) == source).astype(BF)


def row_kernel(g, *refs):
    nc, nr, rows, cols, cpd = g["nc"], g["nr"], g["rows"], g["cols"], g["cpd"]
    xs, qkv, wo, outs, mixed = refs[:nc], refs[nc], refs[nc + 1], refs[nc + 2 : -1], refs[-1]
    tokens, line = rows * nc * cols, nc * cols

    def load():
        parts = [xs[k][i * cols : (i + 1) * cols, :] for i in range(rows) for k in range(nc)]
        return jnp.concatenate(parts, 0).astype(F32)

    n = normalize(load())
    group = min(max(line, 128), tokens)
    mask = None
    if group > line:
        a = lax.broadcasted_iota(jnp.int32, (group, group), 0) // line
        b = lax.broadcasted_iota(jnp.int32, (group, group), 1) // line
        mask = a == b
    width = n.shape[-1]
    head = width // HEADS
    full = dot(n, qkv[...]).astype(BF)
    where = [(slice(t, t + group), h) for h in range(HEADS) for t in range(0, tokens, group)]
    units = [[full[span, j * width + h * head : j * width + (h + 1) * head] for j in range(3)] for span, h in where]
    for (span, h), out in zip(where, attend(units, mask)):
        mixed[span, h * head : (h + 1) * head] = out
    after = (load() + dot(mixed[...], wo[...])).astype(BF)
    o = lax.broadcasted_iota(jnp.int32, (tokens, 1), 0)
    i, jj, rest = o % rows, (o // rows) % cpd, o // (rows * cpd)
    chips = nr // 2
    if len(outs) == nc:
        k, b, q = rest // nr, (rest // chips) % 2, rest % chips
    else:
        k, b, q = rest % nc, rest // (nc * chips), (rest // nc) % chips
    m = 2 * q + b
    source = (i * nc + k) * cols + cpd * jnp.bitwise_xor(m, lax.axis_index("row")) + jj
    moved = dot(one_hot(source, tokens), after).astype(BF)
    each = tokens // len(outs)
    for part, out in enumerate(outs):
        out[...] = moved[part * each : (part + 1) * each, :]


def near(x):
    return pltpu.with_memory_space_constraint(x, pltpu.VMEM)


SMEM_SPEC = pl.BlockSpec(memory_space=pltpu.SMEM)
VMEM_SPEC = pl.BlockSpec(memory_space=pltpu.VMEM)


def call(kernel, ins, outs, scratch, flops, limit=16 << 20):
    moved = sum(a.size * 2 for a in ins) + sum(math.prod(o) * 2 for o in outs)
    small = [a.dtype == jnp.int32 for a in ins]
    return pl.pallas_call(
        kernel,
        in_specs=[SMEM_SPEC if i else VMEM_SPEC for i in small],
        out_specs=[VMEM_SPEC] * len(outs),
        out_shape=[jax.ShapeDtypeStruct(o, BF) for o in outs],
        scratch_shapes=scratch,
        compiler_params=pltpu.CompilerParams(vmem_limit_bytes=limit),
        cost_estimate=pl.CostEstimate(flops=flops, bytes_accessed=moved, transcendentals=0),
    )(*[a if i else near(a) for a, i in zip(ins, small)])


def split_kernel(count, band, offset, latents, *refs):
    outs, sems = refs[:count], refs[count]
    rows = outs[0].shape[0]
    copies = []
    for k in [*range(1, count), 0]:
        at = jnp.bitwise_xor(lax.axis_index("col"), k) * band + offset
        copies.append(pltpu.make_async_copy(latents.at[pl.ds(at, rows)], outs[k], sems.at[k]))
    for copy in copies:
        copy.start()
    for copy in copies:
        copy.wait()


def split(latents, count, band, offset, rows):
    _, cols, width = latents.shape
    return pl.pallas_call(
        functools.partial(split_kernel, count, band, offset),
        in_specs=[pl.BlockSpec(memory_space=pltpu.HBM)],
        out_specs=[VMEM_SPEC] * count,
        out_shape=[pltpu.VMEM((rows, cols, width), BF)] * count,
        scratch_shapes=[pltpu.SemaphoreType.DMA((count,))],
        compiler_params=pltpu.CompilerParams(vmem_limit_bytes=1 << 20),
        cost_estimate=pl.CostEstimate(flops=0, bytes_accessed=4 * count * rows * cols * width, transcendentals=0),
        name="split",
    )(pltpu.with_memory_space_constraint(latents, pltpu.HBM))


def fetch_kernel(count, pieces, *refs):
    ins, outs, sems = refs[:count], refs[count : 2 * count], refs[2 * count]
    copies = []
    for i in range(count):
        size = ins[i].shape[0] // pieces
        for j in range(pieces):
            span = pl.ds(j * size, size)
            copies.append(pltpu.make_async_copy(ins[i].at[span], outs[i].at[span], sems.at[i, j]))
    for copy in copies:
        copy.start()
    for copy in copies:
        copy.wait()


def fetch(weights, pieces=4):
    count = len(weights)
    total = sum(2 * w.size for w in weights)
    return pl.pallas_call(
        functools.partial(fetch_kernel, count, pieces),
        in_specs=[pl.BlockSpec(memory_space=pltpu.HBM)] * count,
        out_specs=[VMEM_SPEC] * count,
        out_shape=[pltpu.VMEM(w.shape, w.dtype) for w in weights],
        scratch_shapes=[pltpu.SemaphoreType.DMA((count, pieces))],
        compiler_params=pltpu.CompilerParams(vmem_limit_bytes=1 << 20),
        cost_estimate=pl.CostEstimate(flops=0, bytes_accessed=2 * total, transcendentals=0),
        name="fetch",
    )(*[pltpu.with_memory_space_constraint(w, pltpu.HBM) for w in weights])


def row_stage(g, parts, slots, row_qkv, row_out):
    tokens = g["rows"] * g["nc"] * g["cols"]
    width = row_out.shape[0]
    return call(
        functools.partial(row_kernel, g),
        [*slots, row_qkv, row_out],
        [(tokens // parts, width)] * parts,
        [pltpu.VMEM((tokens, width), BF)],
        8 * tokens * width * width,
    )


def gather_columns(g, xs, by_row):
    cpd, rows, nr, nc = g["cpd"], g["rows"], g["nr"], g["nc"]
    x = jnp.concatenate([ref[...] for ref in xs], 0)
    tokens = x.shape[0]
    o = lax.broadcasted_iota(jnp.int32, (tokens, 1), 0)
    per = tokens // cpd
    jj, mk, i = o // per, (o % per) // rows, o % rows
    if not by_row:
        mk = (mk % nc) * nr + mk // nc
    return dot(one_hot((mk * cpd + jj) * rows + i, tokens), x)


def project_kernel(g, by_row, *refs):
    xs, w, outs, x_out = refs[:-5], refs[-5], refs[-4:-1], refs[-1]
    x = gather_columns(g, xs, by_row)
    x_out[...] = x.astype(BF)
    n = normalize(x)
    width = n.shape[-1]
    for j, out in enumerate(outs):
        out[...] = dot(n, w[:, j * width : (j + 1) * width]).astype(BF)


def project_stage(g, slots, col_qkv, by_row):
    width = col_qkv.shape[0]
    tokens = sum(a.shape[0] for a in slots)
    return call(
        functools.partial(project_kernel, g, by_row),
        [*slots, col_qkv],
        [(tokens, width)] * 4,
        [],
        6 * tokens * width * width,
    )


def group_kernel(g, members, *refs):
    nr, cpd, nc, rows = g["nr"], g["cpd"], g["nc"], g["rows"]
    old, (wo, up, down) = refs[: 4 * CHUNKS], refs[4 * CHUNKS : 4 * CHUNKS + 3]
    count = len(members)
    outs, (mixed, hidden) = refs[4 * CHUNKS + 3 :][:count], refs[4 * CHUNKS + 3 + count :]
    per = old[0].shape[0] // cpd
    each = per // nr
    width = wo.shape[0]
    head = width // HEADS

    def queries(which, lanes, jj):
        parts = []
        for t in range(CHUNKS):
            for m in members:
                at = jj * per + m * each
                parts.append(old[4 * t + which][at : at + each, lanes])
        return jnp.concatenate(parts, 0)

    def keys(which, lanes, jj):
        return jnp.concatenate([old[4 * t + which][jj * per : (jj + 1) * per, lanes] for t in range(CHUNKS)], 0)

    where = [(jj, slice(h * head, (h + 1) * head)) for h in range(HEADS) for jj in range(cpd)]
    units = [(queries(0, lanes, jj), keys(1, lanes, jj), keys(2, lanes, jj)) for jj, lanes in where]
    size = CHUNKS * count * each
    for (jj, lanes), out in zip(where, attend(units, None)):
        mixed[jj * size : (jj + 1) * size, lanes] = out
    base = jnp.concatenate([queries(3, slice(0, width), jj) for jj in range(cpd)], 0)
    after = (base.astype(F32) + dot(mixed[...], wo[...])).astype(BF)
    n = normalize(after.astype(F32))
    block = min(512, up.shape[1])
    for b in range(0, up.shape[1], block):
        hidden[:, b : b + block] = jax.nn.gelu(dot(n, up[:, b : b + block]), approximate=True).astype(BF)
    result = (after.astype(F32) + dot(hidden[...], down[...])).astype(BF)
    tokens = result.shape[0]
    o = lax.broadcasted_iota(jnp.int32, (tokens, 1), 0)
    jj, i, t = o % cpd, (o // cpd) % rows, (o // (cpd * rows)) % CHUNKS
    c, m = (o // (cpd * rows * CHUNKS)) % nc, o // (cpd * rows * CHUNKS * nc)
    k = jnp.bitwise_xor(c, lax.axis_index("col"))
    source = (((jj * CHUNKS + t) * count + m) * nc + k) * rows + i
    moved = dot(one_hot(source, tokens), result).astype(BF)
    size = tokens // count
    for m in range(count):
        outs[m][...] = moved[m * size : (m + 1) * size, :]


def group_stage(g, members, old, col_out, up_weight, down_weight):
    width, hidden = up_weight.shape
    count = len(members)
    size = CHUNKS * old[0].shape[0] // g["nr"]
    tokens = count * size
    return call(
        functools.partial(group_kernel, g, members),
        [*old, col_out, up_weight, down_weight],
        [(size, width)] * count,
        [pltpu.VMEM((tokens, width), BF), pltpu.VMEM((tokens, hidden), BF)],
        4 * tokens * width * hidden,
    )


def final_kernel(g, *refs):
    nr, cpd, cols, span = g["nr"], g["cpd"], g["cols"], g["span"]
    ins, out = refs[:nr], refs[nr]
    tokens = span * cols
    o = lax.broadcasted_iota(jnp.int32, (tokens, 1), 0)
    w, j = o // cols, o % cols
    m = jnp.bitwise_xor(j // cpd, lax.axis_index("row"))
    pick = one_hot((m * span + w) * cpd + j % cpd, tokens)
    rows = ins[0].shape[0] // cpd
    for a in range(0, rows, span):
        x = jnp.concatenate([ref[a * cpd : (a + span) * cpd, :] for ref in ins], 0)
        out[a * cols : (a + span) * cols, :] = dot(pick, x).astype(BF)


def final_stage(g, slots):
    each, width = slots[0].shape
    total = g["nr"] * each
    (out,) = call(
        functools.partial(final_kernel, g), [*slots], [(total, width)], [], 2 * total * width * g["span"] * g["cols"]
    )
    return out


def swap(x, axis, size, k):
    return x if k == 0 else lax.ppermute(x, axis, [(i, i ^ k) for i in range(size)])


def exchange(parts, axis, order, shift=0):
    n = len(parts)
    size = n << shift
    got = {0: parts[0]}
    for k in order:
        got[k] = swap(parts[k], axis, size, k << shift)
    return [got[k] for k in range(n)]


def deal_kernel(plan, *refs):
    ins, outs = refs[: -len(plan)], refs[-len(plan) :]
    for out, pieces in zip(outs, plan):
        at = 0
        for i, start, size in pieces:
            out[at : at + size, :] = ins[i][start : start + size, :]
            at += size


def deal(ins, plan):
    width = ins[0].shape[1]
    return call(functools.partial(deal_kernel, plan), ins, [(sum(p[2] for p in pieces), width) for pieces in plan], [], 0)


def row_hop(ins, own, sent, cells, nr):
    came = swap(sent, "row", nr, 1)
    chips = nr // 2
    count = len(ins)
    plan = [own(q) + [(count, start, size) for start, size in cells(q)] for q in range(chips)]
    parts = deal([*ins, came], plan)
    return spread(parts, chip_order(nr))


def spread(parts, order):
    n = len(parts)
    got = {0: parts[0]}
    for q in order:
        got[q] = lax.ppermute(parts[q], "row", [(i, i ^ (2 * q)) for i in range(2 * n)])
    return [got[q] for q in range(n)]


def on_device(nr, nc, latents, row_qkv, row_out, col_qkv, col_out, up_weight, down_weight):
    local_rows, cols, width = latents.shape
    band = local_rows // nc
    rows = band // CHUNKS
    cpd = cols // nr
    chips = nr // 2
    cell = rows * cpd
    g = dict(nr=nr, nc=nc, rows=rows, cols=cols, cpd=cpd, span=8)
    z_order = list(range(nc - 1, 0, -1))

    def enter(t, latents):
        slots = split(latents, nc, band, t * rows, rows)
        slots = [a.reshape(rows * cols, width) for a in slots]
        return exchange(slots, "col", z_order)

    first = enter(0, latents)
    weights = fetch([row_qkv, row_out, col_qkv, col_out])
    latents, row_qkv, row_out, col_qkv, col_out = lax.optimization_barrier((latents, *weights))
    second = enter(1, latents)

    parts = row_stage(g, nc, first, row_qkv, row_out)
    up_weight, down_weight = fetch([up_weight, down_weight])
    parts = exchange(parts, "col", z_order)
    half = chips * cell
    (sent,) = deal(parts, [[(k, half, half) for k in range(nc)]])
    slots0 = row_hop(
        parts,
        lambda q: [(k, q * cell, cell) for k in range(nc)],
        sent,
        lambda q: [(k * half + q * cell, cell) for k in range(nc)],
        nr,
    )

    stay, sent = row_stage(g, 2, second, row_qkv, row_out)
    size = nc * cell
    parts = row_hop([stay], lambda q: [(0, q * size, size)], sent, lambda q: [(q * size, size)], nr)
    plan = [[(q, b * size + k * cell, cell) for q in range(chips) for b in range(2)] for k in range(nc)]
    parts = deal(parts, plan)
    slots1 = exchange(parts, "col", z_order)

    old = project_stage(g, slots0, col_qkv, True)
    old += project_stage(g, slots1, col_qkv, False)
    final = [None] * nr
    for members in groups(nr):
        outs = group_stage(g, members, old, col_out, up_weight, down_weight)
        for m, out in zip(members, outs):
            final[m] = swap(out, "row", nr, m)
    return final_stage(g, final).reshape(local_rows, cols, width)


def chip_order(nr):
    return sorted(range(1, nr // 2), key=lambda q: bin(q).count("1"))


def groups(nr):
    near = sorted([*range(2, nr, 2), nr - 1], key=lambda m: bin(m // 2).count("1"))
    return near, [m for m in range(nr - 1, -1, -1) if m not in near]


def solution(mesh):
    in_specs = (P("row", "col", None), P(), P(), P(), P(), P(), P())
    return jax.shard_map(
        functools.partial(on_device, mesh.shape["row"], mesh.shape["col"]),
        mesh=mesh,
        in_specs=in_specs,
        out_specs=P("row", "col", None),
        check_vma=False,
    )
```

```python
import functools
import math

import jax
import jax.numpy as jnp
from jax import lax
from jax.experimental import pallas as pl
from jax.experimental.pallas import tpu as pltpu
from jax.sharding import PartitionSpec as P


HEADS = 8
CHUNKS = 2
PIECES = 4
BF = jnp.bfloat16
F32 = jnp.float32


def normalize(wide):
    return (wide * lax.rsqrt(jnp.mean(wide * wide, -1, keepdims=True) + 1e-06)).astype(BF)


def dot(a, b):
    return jnp.dot(a, b, preferred_element_type=F32)


def dot_t(a, b):
    return lax.dot_general(a, b, (((1,), (1,)), ((), ())), preferred_element_type=F32)


def attend(units, mask):
    scores = [dot_t(q, k) for q, k, _ in units]
    weights = []
    for s, (q, _, _) in zip(scores, units):
        gain = math.log2(math.e) / math.sqrt(q.shape[-1])
        if mask is not None:
            s = jnp.where(mask, s, -1e30)
        weights.append(jnp.exp2((s - jnp.max(s, -1, keepdims=True)) * gain).astype(BF))
    outs = []
    for e, (_, _, v) in zip(weights, units):
        both = dot(e, jnp.concatenate([v, jnp.ones_like(v)], -1))
        width = v.shape[-1]
        outs.append((both[:, :width] / both[:, width:]).astype(BF))
    return outs


def one_hot(source, size):
    return (lax.broadcasted_iota(jnp.int32, (source.shape[0], size), 1) == source).astype(BF)


def row_kernel(g, *refs):
    nc, nr, rows, cols, cpd = g["nc"], g["nr"], g["rows"], g["cols"], g["cpd"]
    xs, qkv, wo, outs, mixed = refs[:nc], refs[nc], refs[nc + 1], refs[nc + 2 : -1], refs[-1]
    tokens, line = rows * nc * cols, nc * cols

    def load():
        parts = [xs[k][i * cols : (i + 1) * cols, :] for i in range(rows) for k in range(nc)]
        return jnp.concatenate(parts, 0).astype(F32)

    n = normalize(load())
    group = min(max(line, 128), tokens)
    mask = None
    if group > line:
        a = lax.broadcasted_iota(jnp.int32, (group, group), 0) // line
        b = lax.broadcasted_iota(jnp.int32, (group, group), 1) // line
        mask = a == b
    width = n.shape[-1]
    head = width // HEADS
    full = dot(n, qkv[...]).astype(BF)
    where = [(slice(t, t + group), h) for h in range(HEADS) for t in range(0, tokens, group)]
    units = [[full[span, j * width + h * head : j * width + (h + 1) * head] for j in range(3)] for span, h in where]
    for (span, h), out in zip(where, attend(units, mask)):
        mixed[span, h * head : (h + 1) * head] = out
    after = (load() + dot(mixed[...], wo[...])).astype(BF)
    o = lax.broadcasted_iota(jnp.int32, (tokens, 1), 0)
    i, jj, rest = o % rows, (o // rows) % cpd, o // (rows * cpd)
    if len(outs) == nc:
        k, b, q = rest // nr, (rest // (nr // 2)) % 2, rest % (nr // 2)
        r = jnp.bitwise_xor(2 * q + b, lax.axis_index("row"))
    else:
        r, k = rest // nc, jnp.bitwise_xor(rest % nc, lax.axis_index("col"))
    source = (i * nc + k) * cols + cpd * r + jj
    moved = dot(one_hot(source, tokens), after).astype(BF)
    each = tokens // len(outs)
    for part, out in enumerate(outs):
        out[...] = moved[part * each : (part + 1) * each, :]


def near(x):
    return pltpu.with_memory_space_constraint(x, pltpu.VMEM)


HBM_SPEC = pl.BlockSpec(memory_space=pltpu.HBM)
VMEM_SPEC = pl.BlockSpec(memory_space=pltpu.VMEM)


def call(kernel, ins, outs, scratch, flops, limit=16 << 20, far=False):
    moved = sum(a.size * 2 for a in ins) + sum(math.prod(o) * 2 for o in outs)
    return pl.pallas_call(
        kernel,
        in_specs=[VMEM_SPEC] * len(ins),
        out_specs=[VMEM_SPEC] * len(outs),
        out_shape=[jax.ShapeDtypeStruct(o, BF) for o in outs],
        scratch_shapes=scratch,
        compiler_params=pltpu.CompilerParams(vmem_limit_bytes=limit),
        cost_estimate=pl.CostEstimate(flops=flops, bytes_accessed=moved, transcendentals=0),
    )(*[a if far else near(a) for a in ins])


def split_kernel(count, band, offset, latents, *refs):
    outs, sems = refs[:count], refs[count]
    rows = outs[0].shape[0]
    copies = []
    for k in [*range(1, count), 0]:
        at = jnp.bitwise_xor(lax.axis_index("col"), k) * band + offset
        copies.append(pltpu.make_async_copy(latents.at[pl.ds(at, rows)], outs[k], sems.at[k]))
    for copy in copies:
        copy.start()
    for copy in copies:
        copy.wait()


def split(latents, count, band, offset, rows):
    _, cols, width = latents.shape
    return pl.pallas_call(
        functools.partial(split_kernel, count, band, offset),
        in_specs=[pl.BlockSpec(memory_space=pltpu.HBM)],
        out_specs=[VMEM_SPEC] * count,
        out_shape=[pltpu.VMEM((rows, cols, width), BF)] * count,
        scratch_shapes=[pltpu.SemaphoreType.DMA((count,))],
        compiler_params=pltpu.CompilerParams(vmem_limit_bytes=1 << 20),
        cost_estimate=pl.CostEstimate(flops=0, bytes_accessed=4 * count * rows * cols * width, transcendentals=0),
        name="split",
    )(pltpu.with_memory_space_constraint(latents, pltpu.HBM))


def fetch_kernel(count, pieces, *refs):
    ins, outs, sems = refs[:count], refs[count : 2 * count], refs[2 * count]
    copies = []
    for i in range(count):
        size = ins[i].shape[0] // pieces
        for j in range(pieces):
            span = pl.ds(j * size, size)
            copies.append(pltpu.make_async_copy(ins[i].at[span], outs[i].at[span], sems.at[i, j]))
    for copy in copies:
        copy.start()
    for copy in copies:
        copy.wait()


def fetch(weights, pieces=4):
    count = len(weights)
    total = sum(2 * w.size for w in weights)
    return pl.pallas_call(
        functools.partial(fetch_kernel, count, pieces),
        in_specs=[pl.BlockSpec(memory_space=pltpu.HBM)] * count,
        out_specs=[VMEM_SPEC] * count,
        out_shape=[pltpu.VMEM(w.shape, w.dtype) for w in weights],
        scratch_shapes=[pltpu.SemaphoreType.DMA((count, pieces))],
        compiler_params=pltpu.CompilerParams(vmem_limit_bytes=1 << 20),
        cost_estimate=pl.CostEstimate(flops=0, bytes_accessed=2 * total, transcendentals=0),
        name="fetch",
    )(*[pltpu.with_memory_space_constraint(w, pltpu.HBM) for w in weights])


def row_stage(g, parts, slots, row_qkv, row_out):
    tokens = g["rows"] * g["nc"] * g["cols"]
    width = row_out.shape[0]
    return call(
        functools.partial(row_kernel, g),
        [*slots, row_qkv, row_out],
        [(tokens // parts, width)] * parts,
        [pltpu.VMEM((tokens, width), BF)],
        8 * tokens * width * width,
    )


def gather_columns(g, xs, by_row):
    cpd, rows, nc = g["cpd"], g["rows"], g["nc"]
    x = jnp.concatenate([ref[...] for ref in xs], 0)
    tokens = x.shape[0]
    o = lax.broadcasted_iota(jnp.int32, (tokens, 1), 0)
    per = tokens // cpd
    jj, mk, i = o // per, (o % per) // rows, o % rows
    if not by_row:
        r, c = lax.axis_index("row"), lax.axis_index("col")
        mk = jnp.bitwise_xor(mk // nc, r) * nc + jnp.bitwise_xor(mk % nc, c)
    return dot(one_hot((mk * cpd + jj) * rows + i, tokens), x)


def group_kernel(g, members, *refs):
    old, (wo, up, down) = refs[: 4 * CHUNKS], refs[4 * CHUNKS : 4 * CHUNKS + 3]
    outs, (mixed, hidden) = refs[4 * CHUNKS + 3 : -2], refs[-2:]
    group_body(g, members, old, wo, outs, mixed, lambda: None, lambda after: feed_forward(after, up, down, hidden))


def group_body(g, members, old, wo, outs, mixed, ready, finish):
    nr, cpd, nc, rows = g["nr"], g["cpd"], g["nc"], g["rows"]
    count = len(members)
    per = old[0].shape[0] // cpd
    each = per // nr
    width = wo.shape[0]
    head = width // HEADS

    def queries(which, lanes, jj):
        parts = []
        for t in range(CHUNKS):
            for m in members:
                at = jj * per + m * each
                parts.append(old[4 * t + which][at : at + each, lanes])
        return jnp.concatenate(parts, 0)

    def keys(which, lanes, jj):
        return jnp.concatenate([old[4 * t + which][jj * per : (jj + 1) * per, lanes] for t in range(CHUNKS)], 0)

    where = [(jj, slice(h * head, (h + 1) * head)) for h in range(HEADS) for jj in range(cpd)]
    units = [(queries(0, lanes, jj), keys(1, lanes, jj), keys(2, lanes, jj)) for jj, lanes in where]
    size = CHUNKS * count * each
    for (jj, lanes), out in zip(where, attend(units, None)):
        mixed[jj * size : (jj + 1) * size, lanes] = out
    ready()
    base = jnp.concatenate([queries(3, slice(0, width), jj) for jj in range(cpd)], 0)
    after = (base.astype(F32) + dot(mixed[...], wo[...])).astype(BF)
    after = finish(after)
    tokens = after.shape[0]
    o = lax.broadcasted_iota(jnp.int32, (tokens, 1), 0)
    jj, i, t = o % cpd, (o // cpd) % rows, (o // (cpd * rows)) % CHUNKS
    c, m = (o // (cpd * rows * CHUNKS)) % nc, o // (cpd * rows * CHUNKS * nc)
    k = jnp.bitwise_xor(c, lax.axis_index("col"))
    source = (((jj * CHUNKS + t) * count + m) * nc + k) * rows + i
    moved = dot(one_hot(source, tokens), after).astype(BF)
    size = tokens // count
    for m in range(count):
        outs[m][...] = moved[m * size : (m + 1) * size, :]


def group_stage(g, members, old, col_out, up_weight, down_weight):
    width, size = up_weight.shape
    count = len(members)
    each = CHUNKS * old[0].shape[0] // g["nr"]
    tokens = count * each
    return call(
        functools.partial(group_kernel, g, members),
        [*old, col_out, up_weight, down_weight],
        [(each, width)] * count,
        [pltpu.VMEM((tokens, width), BF), pltpu.VMEM((tokens, size), BF)],
        4 * tokens * width * size,
    )


def finish_kernel(g, members, counts, *refs):
    n_x = sum(counts)
    xs, far_qkv, far_weights, rest = refs[:n_x], refs[n_x], refs[n_x + 1 : n_x + 4], refs[n_x + 4 :]
    old, weights, outs = rest[: 4 * CHUNKS], rest[4 * CHUNKS : 4 * CHUNKS + 3], rest[4 * CHUNKS + 3 : -3]
    qkv, mixed, sems = rest[-3:]
    width = xs[0].shape[1]
    sources = [far_qkv.at[:, pl.ds(j * width, width)] for j in range(3)] + list(far_weights)
    targets = [qkv.at[:, pl.ds(j * width, width)] for j in range(3)] + list(weights)

    def pieces(i):
        size = sources[i].shape[0] // PIECES
        spans = [pl.ds(a * size, size) for a in range(PIECES)]
        return [pltpu.make_async_copy(sources[i].at[a], targets[i].at[a], sems.at[i, p]) for p, a in enumerate(spans)]

    def begin(*which):
        for i in which:
            for copy in pieces(i):
                copy.start()

    def arrived(i):
        for copy in pieces(i):
            copy.wait()

    begin(0, 1)
    normed, at = [], 0
    for t, count in enumerate(counts):
        x = gather_columns(g, xs[at : at + count], t < CHUNKS - 1)
        old[4 * t + 3][...] = x.astype(BF)
        normed.append(normalize(x))
        at += count
    n = jnp.concatenate(normed, 0)
    size = n.shape[0] // CHUNKS
    for j in range(3):
        arrived(j)
        begin(*([2], [3, 4], [5])[j])
        value = dot(n, qkv[:, j * width : (j + 1) * width]).astype(BF)
        for t in range(CHUNKS):
            old[4 * t + j][...] = value[t * size : (t + 1) * size, :]

    group_body(g, members, old, weights[0], outs, mixed, lambda: arrived(3), lambda after: after)
    arrived(4)
    arrived(5)


def finish_stage(g, members, slots, col_qkv, col_out, up_weight, down_weight):
    width = col_out.shape[0]
    count = len(members)
    chunk = sum(a.shape[0] for a in slots[0])
    tokens = count * CHUNKS * chunk // g["nr"]
    far = [col_qkv, col_out, up_weight, down_weight]
    flat = [a for part in slots for a in part]
    kept = [(chunk, width)] * (4 * CHUNKS) + [col_out.shape, up_weight.shape, down_weight.shape]
    outs = pl.pallas_call(
        functools.partial(finish_kernel, g, members, [len(part) for part in slots]),
        in_specs=[VMEM_SPEC] * len(flat) + [HBM_SPEC] * len(far),
        out_specs=[VMEM_SPEC] * (len(kept) + count),
        out_shape=[pltpu.VMEM(shape, BF) for shape in kept] + [jax.ShapeDtypeStruct((tokens // count, width), BF)] * count,
        scratch_shapes=[
            pltpu.VMEM(col_qkv.shape, BF),
            pltpu.VMEM((tokens, width), BF),
            pltpu.SemaphoreType.DMA((6, PIECES)),
        ],
        compiler_params=pltpu.CompilerParams(vmem_limit_bytes=28 << 20),
        cost_estimate=pl.CostEstimate(flops=16 * tokens * width * width, bytes_accessed=2 * sum(a.size for a in far), transcendentals=0),
        name="finish_stage",
    )(*[near(a) for a in flat], *[pltpu.with_memory_space_constraint(a, pltpu.HBM) for a in far])
    return outs[: 4 * CHUNKS], outs[4 * CHUNKS : 4 * CHUNKS + 3], outs[4 * CHUNKS + 3 :]


def feed_forward(x, up, down, hidden):
    n = normalize(x.astype(F32))
    block = min(512, up.shape[1])
    for b in range(0, up.shape[1], block):
        hidden[:, b : b + block] = jax.nn.gelu(dot(n, up[:, b : b + block]), approximate=True).astype(BF)
    return (x.astype(F32) + dot(hidden[...], down[...])).astype(BF)


def ffn_kernel(*refs):
    slots, (up, down, out, hidden) = refs[:-4], refs[-4:]
    out[...] = feed_forward(jnp.concatenate([ref[...] for ref in slots], 0), up, down, hidden)


def ffn_stage(slots, up_weight, down_weight):
    width, size = up_weight.shape
    tokens = sum(a.shape[0] for a in slots)
    (out,) = call(
        ffn_kernel,
        [*slots, up_weight, down_weight],
        [(tokens, width)],
        [pltpu.VMEM((tokens, size), BF)],
        4 * tokens * width * size,
    )
    return out


def final_kernel(g, order, *refs):
    cpd, cols, span = g["cpd"], g["cols"], g["span"]
    first, slots, (out, held, sems) = refs[0], refs[1:-3], refs[-3:]
    tokens = span * cols
    each = slots[0].shape[0]
    o = lax.broadcasted_iota(jnp.int32, (tokens, 1), 0)
    w, j = o // cols, o % cols
    m = jnp.bitwise_xor(j // cpd, lax.axis_index("row"))
    pick = one_hot((m * span + w) * cpd + j % cpd, tokens)
    half = len(order) - len(slots)
    copies = []
    for a in range(0, each // cpd, span):
        parts = []
        for m in range(len(order)):
            i = order.index(m)
            at, ref = (i * each, first) if i < half else (0, slots[i - half])
            parts.append(ref[at + a * cpd : at + (a + span) * cpd, :])
        held[a * cols : (a + span) * cols, :] = dot(pick, jnp.concatenate(parts, 0)).astype(BF)
        rows = pl.ds(a * cols, span * cols)
        copies.append(pltpu.make_async_copy(held.at[rows], out.at[rows], sems.at[len(copies)]))
        copies[-1].start()
    for copy in copies:
        copy.wait()


def final_stage(g, order, first, slots):
    width = first.shape[1]
    tokens = first.shape[0] + sum(a.shape[0] for a in slots)
    return pl.pallas_call(
        functools.partial(final_kernel, g, order),
        in_specs=[VMEM_SPEC] * (1 + len(slots)),
        out_specs=HBM_SPEC,
        out_shape=pltpu.HBM((tokens, width), BF),
        scratch_shapes=[
            pltpu.VMEM((tokens, width), BF),
            pltpu.SemaphoreType.DMA((tokens // (g["span"] * g["cols"]),)),
        ],
        compiler_params=pltpu.CompilerParams(vmem_limit_bytes=8 << 20),
        cost_estimate=pl.CostEstimate(flops=0, bytes_accessed=4 * tokens * width, transcendentals=0),
        name="final_stage",
    )(*[near(a) for a in [first, *slots]])


def swap(x, axis, size, k):
    return x if k == 0 else lax.ppermute(x, axis, [(i, i ^ k) for i in range(size)])


def exchange(parts, axis, order, shift=0):
    n = len(parts)
    size = n << shift
    got = {0: parts[0]}
    for k in order:
        got[k] = swap(parts[k], axis, size, k << shift)
    return [got[k] for k in range(n)]


def deal_kernel(plan, *refs):
    ins, outs = refs[: -len(plan)], refs[-len(plan) :]
    for out, pieces in zip(outs, plan):
        at = 0
        for i, start, size in pieces:
            out[at : at + size, :] = ins[i][start : start + size, :]
            at += size


def deal(ins, plan):
    width = ins[0].shape[1]
    return call(functools.partial(deal_kernel, plan), ins, [(sum(p[2] for p in pieces), width) for pieces in plan], [], 0, far=True)


def row_hop(ins, own, sent, cells, nr):
    came = swap(sent, "row", nr, 1)
    chips = nr // 2
    count = len(ins)
    plan = [own(q) + [(count, start, size) for start, size in cells(q)] for q in range(chips)]
    parts = deal([*ins, came], plan)
    return spread(parts, chip_order(nr))


def spread(parts, order):
    n = len(parts)
    got = {0: parts[0]}
    for q in order:
        got[q] = lax.ppermute(parts[q], "row", [(i, i ^ (2 * q)) for i in range(2 * n)])
    return [got[q] for q in range(n)]


def on_device(nr, nc, latents, row_qkv, row_out, col_qkv, col_out, up_weight, down_weight):
    local_rows, cols, width = latents.shape
    band = local_rows // nc
    rows = band // CHUNKS
    cpd = cols // nr
    chips = nr // 2
    cell = rows * cpd
    g = dict(nr=nr, nc=nc, rows=rows, cols=cols, cpd=cpd, span=8)
    z_order = list(range(nc - 1, 0, -1))

    def enter(t, latents):
        slots = split(latents, nc, band, t * rows, rows)
        slots = [a.reshape(rows * cols, width) for a in slots]
        return exchange(slots, "col", z_order)

    first = enter(0, latents)
    weights = fetch([row_qkv, row_out])
    latents, row_qkv, row_out = lax.optimization_barrier((latents, *weights))
    second = enter(1, latents)

    parts = row_stage(g, nc, first, row_qkv, row_out)
    parts = exchange(parts, "col", z_order)
    half = chips * cell
    (sent,) = deal(parts, [[(k, half, half) for k in range(nc)]])
    slots0 = row_hop(
        parts,
        lambda q: [(k, q * cell, cell) for k in range(nc)],
        sent,
        lambda q: [(k * half + q * cell, cell) for k in range(nc)],
        nr,
    )

    (parts,) = row_stage(g, 1, second, row_qkv, row_out)
    parts = parts.reshape(nr * nc, cell, width)
    parts = lax.all_to_all(parts, ("row", "col"), split_axis=0, concat_axis=0, tiled=True)
    slots1 = parts.reshape(nr * nc * cell, width)

    came = {}
    near_half, far_half = groups(nr)
    for b, members in enumerate((near_half, far_half)):
        if b == 0:
            ins = [slots0, [slots1]]
            old, weights, outs = finish_stage(g, members, ins, col_qkv, col_out, up_weight, down_weight)
        else:
            outs = group_stage(g, members, old, *weights)
        for m, out in zip(members, outs):
            came[m] = swap(out, "row", nr, m)
    done = ffn_stage([came[m] for m in near_half], *weights[1:])
    out = final_stage(g, near_half + far_half, done, [came[m] for m in far_half])
    return out.reshape(local_rows, cols, width)


def chip_order(nr):
    return sorted(range(1, nr // 2), key=lambda q: bin(q).count("1"))


def groups(nr):
    near = sorted([*range(2, nr, 2), nr - 1], key=lambda m: bin(m // 2).count("1"))
    return near, [m for m in range(nr - 1, -1, -1) if m not in near]


def solution(mesh):
    in_specs = (P("row", "col", None), P(), P(), P(), P(), P(), P())
    return jax.shard_map(
        functools.partial(on_device, mesh.shape["row"], mesh.shape["col"]),
        mesh=mesh,
        in_specs=in_specs,
        out_specs=P("row", "col", None),
        check_vma=False,
    )
```

```python
import functools
import math

import jax
import jax.numpy as jnp
from jax import lax
from jax.experimental import pallas as pl
from jax.experimental.pallas import tpu as pltpu
from jax.sharding import PartitionSpec as P


HEADS = 8
CHUNKS = 2
PIECES = 2
BF = jnp.bfloat16
F32 = jnp.float32


def normalize(wide):
    return (wide * lax.rsqrt(jnp.mean(wide * wide, -1, keepdims=True) + 1e-06)).astype(BF)


def dot(a, b):
    return jnp.dot(a, b, preferred_element_type=F32)


def dot_t(a, b):
    return lax.dot_general(a, b, (((1,), (1,)), ((), ())), preferred_element_type=F32)


def attend(units, mask):
    scores = [dot_t(q, k) for q, k, _ in units]
    weights = []
    for s, (q, _, _) in zip(scores, units):
        gain = math.log2(math.e) / math.sqrt(q.shape[-1])
        if mask is not None:
            s = jnp.where(mask, s, -1e30)
        weights.append(jnp.exp2((s - jnp.max(s, -1, keepdims=True)) * gain).astype(BF))
    outs = []
    for e, (_, _, v) in zip(weights, units):
        both = dot(e, jnp.concatenate([v, jnp.ones_like(v)], -1))
        width = v.shape[-1]
        outs.append((both[:, :width] / both[:, width:]).astype(BF))
    return outs


def one_hot(source, size):
    return (lax.broadcasted_iota(jnp.int32, (source.shape[0], size), 1) == source).astype(BF)


def row_kernel(g, *refs):
    nc, nr, rows, cols, cpd = g["nc"], g["nr"], g["rows"], g["cols"], g["cpd"]
    xs, qkv, wo, outs, mixed = refs[:nc], refs[nc], refs[nc + 1], refs[nc + 2 : -1], refs[-1]
    tokens, line = rows * nc * cols, nc * cols

    def load():
        parts = [xs[k][i * cols : (i + 1) * cols, :] for i in range(rows) for k in range(nc)]
        return jnp.concatenate(parts, 0).astype(F32)

    n = normalize(load())
    group = min(max(line, 128), tokens)
    mask = None
    if group > line:
        a = lax.broadcasted_iota(jnp.int32, (group, group), 0) // line
        b = lax.broadcasted_iota(jnp.int32, (group, group), 1) // line
        mask = a == b
    width = n.shape[-1]
    head = width // HEADS
    full = dot(n, qkv[...]).astype(BF)
    where = [(slice(t, t + group), h) for h in range(HEADS) for t in range(0, tokens, group)]
    units = [[full[span, j * width + h * head : j * width + (h + 1) * head] for j in range(3)] for span, h in where]
    for (span, h), out in zip(where, attend(units, mask)):
        mixed[span, h * head : (h + 1) * head] = out
    after = (load() + dot(mixed[...], wo[...])).astype(BF)
    o = lax.broadcasted_iota(jnp.int32, (tokens, 1), 0)
    i, jj, rest = o % rows, (o // rows) % cpd, o // (rows * cpd)
    if len(outs) == nc:
        k, b, q = rest // nr, (rest // (nr // 2)) % 2, rest % (nr // 2)
        r = jnp.bitwise_xor(2 * q + b, lax.axis_index("row"))
    else:
        r, k = rest // nc, jnp.bitwise_xor(rest % nc, lax.axis_index("col"))
    source = (i * nc + k) * cols + cpd * r + jj
    moved = dot(one_hot(source, tokens), after).astype(BF)
    each = tokens // len(outs)
    for part, out in enumerate(outs):
        out[...] = moved[part * each : (part + 1) * each, :]


def near(x):
    return pltpu.with_memory_space_constraint(x, pltpu.VMEM)


HBM_SPEC = pl.BlockSpec(memory_space=pltpu.HBM)
VMEM_SPEC = pl.BlockSpec(memory_space=pltpu.VMEM)


def call(kernel, ins, outs, scratch, flops, limit=16 << 20, far=False):
    moved = sum(a.size * 2 for a in ins) + sum(math.prod(o) * 2 for o in outs)
    return pl.pallas_call(
        kernel,
        in_specs=[VMEM_SPEC] * len(ins),
        out_specs=[VMEM_SPEC] * len(outs),
        out_shape=[jax.ShapeDtypeStruct(o, BF) for o in outs],
        scratch_shapes=scratch,
        compiler_params=pltpu.CompilerParams(vmem_limit_bytes=limit),
        cost_estimate=pl.CostEstimate(flops=flops, bytes_accessed=moved, transcendentals=0),
    )(*[a if far else near(a) for a in ins])


def split_kernel(count, band, offset, latents, *refs):
    outs, sems = refs[:count], refs[count]
    rows = outs[0].shape[0]
    copies = []
    for k in [*range(1, count), 0]:
        at = jnp.bitwise_xor(lax.axis_index("col"), k) * band + offset
        copies.append(pltpu.make_async_copy(latents.at[pl.ds(at, rows)], outs[k], sems.at[k]))
    for copy in copies:
        copy.start()
    for copy in copies:
        copy.wait()


def split(latents, count, band, offset, rows):
    _, cols, width = latents.shape
    return pl.pallas_call(
        functools.partial(split_kernel, count, band, offset),
        in_specs=[pl.BlockSpec(memory_space=pltpu.HBM)],
        out_specs=[VMEM_SPEC] * count,
        out_shape=[pltpu.VMEM((rows, cols, width), BF)] * count,
        scratch_shapes=[pltpu.SemaphoreType.DMA((count,))],
        compiler_params=pltpu.CompilerParams(vmem_limit_bytes=1 << 20),
        cost_estimate=pl.CostEstimate(flops=0, bytes_accessed=4 * count * rows * cols * width, transcendentals=0),
        name="split",
    )(pltpu.with_memory_space_constraint(latents, pltpu.HBM))


def fetch_kernel(count, pieces, *refs):
    ins, outs, sems = refs[:count], refs[count : 2 * count], refs[2 * count]
    copies = []
    for i in range(count):
        size = ins[i].shape[0] // pieces
        for j in range(pieces):
            span = pl.ds(j * size, size)
            copies.append(pltpu.make_async_copy(ins[i].at[span], outs[i].at[span], sems.at[i, j]))
    for copy in copies:
        copy.start()
    for copy in copies:
        copy.wait()


def fetch(weights, pieces=4):
    count = len(weights)
    total = sum(2 * w.size for w in weights)
    return pl.pallas_call(
        functools.partial(fetch_kernel, count, pieces),
        in_specs=[pl.BlockSpec(memory_space=pltpu.HBM)] * count,
        out_specs=[VMEM_SPEC] * count,
        out_shape=[pltpu.VMEM(w.shape, w.dtype) for w in weights],
        scratch_shapes=[pltpu.SemaphoreType.DMA((count, pieces))],
        compiler_params=pltpu.CompilerParams(vmem_limit_bytes=1 << 20),
        cost_estimate=pl.CostEstimate(flops=0, bytes_accessed=2 * total, transcendentals=0),
        name="fetch",
    )(*[pltpu.with_memory_space_constraint(w, pltpu.HBM) for w in weights])


def row_stage(g, parts, slots, row_qkv, row_out):
    tokens = g["rows"] * g["nc"] * g["cols"]
    width = row_out.shape[0]
    return call(
        functools.partial(row_kernel, g),
        [*slots, row_qkv, row_out],
        [(tokens // parts, width)] * parts,
        [pltpu.VMEM((tokens, width), BF)],
        8 * tokens * width * width,
    )


def gather_columns(g, xs, by_row):
    cpd, rows, nc = g["cpd"], g["rows"], g["nc"]
    x = jnp.concatenate([ref[...] for ref in xs], 0)
    tokens = x.shape[0]
    o = lax.broadcasted_iota(jnp.int32, (tokens, 1), 0)
    per = tokens // cpd
    jj, mk, i = o // per, (o % per) // rows, o % rows
    if not by_row:
        r, c = lax.axis_index("row"), lax.axis_index("col")
        mk = jnp.bitwise_xor(mk // nc, r) * nc + jnp.bitwise_xor(mk % nc, c)
    return dot(one_hot((mk * cpd + jj) * rows + i, tokens), x)


def group_kernel(g, members, *refs):
    old, (wo, up, down) = refs[: 4 * CHUNKS], refs[4 * CHUNKS : 4 * CHUNKS + 3]
    outs, (mixed, hidden) = refs[4 * CHUNKS + 3 : -2], refs[-2:]
    group_body(g, members, old, wo, outs, mixed, lambda: None, lambda after: feed_forward(after, up, down, hidden))


def group_body(g, members, old, wo, outs, mixed, ready, finish):
    nr, cpd, nc, rows = g["nr"], g["cpd"], g["nc"], g["rows"]
    count = len(members)
    per = old[0].shape[0] // cpd
    each = per // nr
    width = wo.shape[0]
    head = width // HEADS

    def queries(which, lanes, jj):
        parts = []
        for t in range(CHUNKS):
            for m in members:
                at = jj * per + m * each
                parts.append(old[4 * t + which][at : at + each, lanes])
        return jnp.concatenate(parts, 0)

    def keys(which, lanes, jj):
        return jnp.concatenate([old[4 * t + which][jj * per : (jj + 1) * per, lanes] for t in range(CHUNKS)], 0)

    where = [(jj, slice(h * head, (h + 1) * head)) for h in range(HEADS) for jj in range(cpd)]
    units = [(queries(0, lanes, jj), keys(1, lanes, jj), keys(2, lanes, jj)) for jj, lanes in where]
    size = CHUNKS * count * each
    for (jj, lanes), out in zip(where, attend(units, None)):
        mixed[jj * size : (jj + 1) * size, lanes] = out
    ready()
    base = jnp.concatenate([queries(3, slice(0, width), jj) for jj in range(cpd)], 0)
    after = (base.astype(F32) + dot(mixed[...], wo[...])).astype(BF)
    after = finish(after)
    tokens = after.shape[0]
    o = lax.broadcasted_iota(jnp.int32, (tokens, 1), 0)
    jj, i, t = o % cpd, (o // cpd) % rows, (o // (cpd * rows)) % CHUNKS
    c, m = (o // (cpd * rows * CHUNKS)) % nc, o // (cpd * rows * CHUNKS * nc)
    k = jnp.bitwise_xor(c, lax.axis_index("col"))
    source = (((jj * CHUNKS + t) * count + m) * nc + k) * rows + i
    moved = dot(one_hot(source, tokens), after).astype(BF)
    size = tokens // count
    for m in range(count):
        outs[m][...] = moved[m * size : (m + 1) * size, :]


def group_stage(g, members, old, col_out, up_weight, down_weight):
    width, size = up_weight.shape
    count = len(members)
    each = CHUNKS * old[0].shape[0] // g["nr"]
    tokens = count * each
    return call(
        functools.partial(group_kernel, g, members),
        [*old, col_out, up_weight, down_weight],
        [(each, width)] * count,
        [pltpu.VMEM((tokens, width), BF), pltpu.VMEM((tokens, size), BF)],
        4 * tokens * width * size,
    )


def finish_kernel(g, members, counts, *refs):
    n_x = sum(counts)
    xs, far_qkv, far_weights, rest = refs[:n_x], refs[n_x], refs[n_x + 1 : n_x + 4], refs[n_x + 4 :]
    old, weights, outs = rest[: 4 * CHUNKS], rest[4 * CHUNKS : 4 * CHUNKS + 3], rest[4 * CHUNKS + 3 : -3]
    qkv, mixed, sems = rest[-3:]
    width = xs[0].shape[1]
    sources = [far_qkv.at[:, pl.ds(j * width, width)] for j in range(3)] + list(far_weights)
    targets = [qkv.at[:, pl.ds(j * width, width)] for j in range(3)] + list(weights)

    def pieces(i):
        size = sources[i].shape[0] // PIECES
        spans = [pl.ds(a * size, size) for a in range(PIECES)]
        return [pltpu.make_async_copy(sources[i].at[a], targets[i].at[a], sems.at[i, p]) for p, a in enumerate(spans)]

    def begin(*which):
        for i in which:
            for copy in pieces(i):
                copy.start()

    def arrived(i):
        for copy in pieces(i):
            copy.wait()

    begin(0, 1)
    normed, at = [], 0
    for t, count in enumerate(counts):
        x = gather_columns(g, xs[at : at + count], t < CHUNKS - 1)
        old[4 * t + 3][...] = x.astype(BF)
        normed.append(normalize(x))
        at += count
    n = jnp.concatenate(normed, 0)
    size = n.shape[0] // CHUNKS
    for j in range(3):
        arrived(j)
        begin(*([2], [3, 4], [5])[j])
        value = dot(n, qkv[:, j * width : (j + 1) * width]).astype(BF)
        for t in range(CHUNKS):
            old[4 * t + j][...] = value[t * size : (t + 1) * size, :]

    group_body(g, members, old, weights[0], outs, mixed, lambda: arrived(3), lambda after: after)
    arrived(4)
    arrived(5)


def finish_stage(g, members, slots, col_qkv, col_out, up_weight, down_weight):
    width = col_out.shape[0]
    count = len(members)
    chunk = sum(a.shape[0] for a in slots[0])
    tokens = count * CHUNKS * chunk // g["nr"]
    far = [col_qkv, col_out, up_weight, down_weight]
    flat = [a for part in slots for a in part]
    kept = [(chunk, width)] * (4 * CHUNKS) + [col_out.shape, up_weight.shape, down_weight.shape]
    outs = pl.pallas_call(
        functools.partial(finish_kernel, g, members, [len(part) for part in slots]),
        in_specs=[VMEM_SPEC] * len(flat) + [HBM_SPEC] * len(far),
        out_specs=[VMEM_SPEC] * (len(kept) + count),
        out_shape=[pltpu.VMEM(shape, BF) for shape in kept] + [jax.ShapeDtypeStruct((tokens // count, width), BF)] * count,
        scratch_shapes=[
            pltpu.VMEM(col_qkv.shape, BF),
            pltpu.VMEM((tokens, width), BF),
            pltpu.SemaphoreType.DMA((6, PIECES)),
        ],
        compiler_params=pltpu.CompilerParams(vmem_limit_bytes=28 << 20),
        cost_estimate=pl.CostEstimate(flops=16 * tokens * width * width, bytes_accessed=2 * sum(a.size for a in far), transcendentals=0),
        name="finish_stage",
    )(*[near(a) for a in flat], *[pltpu.with_memory_space_constraint(a, pltpu.HBM) for a in far])
    return outs[: 4 * CHUNKS], outs[4 * CHUNKS : 4 * CHUNKS + 3], outs[4 * CHUNKS + 3 :]


def feed_forward(x, up, down, hidden):
    n = normalize(x.astype(F32))
    block = min(512, up.shape[1])
    for b in range(0, up.shape[1], block):
        hidden[:, b : b + block] = jax.nn.gelu(dot(n, up[:, b : b + block]), approximate=True).astype(BF)
    return (x.astype(F32) + dot(hidden[...], down[...])).astype(BF)


def ffn_kernel(*refs):
    slots, (up, down, out, hidden) = refs[:-4], refs[-4:]
    out[...] = feed_forward(jnp.concatenate([ref[...] for ref in slots], 0), up, down, hidden)


def ffn_stage(slots, up_weight, down_weight):
    width, size = up_weight.shape
    tokens = sum(a.shape[0] for a in slots)
    (out,) = call(
        ffn_kernel,
        [*slots, up_weight, down_weight],
        [(tokens, width)],
        [pltpu.VMEM((tokens, size), BF)],
        4 * tokens * width * size,
    )
    return out


def final_kernel(g, order, *refs):
    cpd, cols, span = g["cpd"], g["cols"], g["span"]
    first, slots, (out, held, sems) = refs[0], refs[1:-3], refs[-3:]
    tokens = span * cols
    each = slots[0].shape[0]
    o = lax.broadcasted_iota(jnp.int32, (tokens, 1), 0)
    w, j = o // cols, o % cols
    m = jnp.bitwise_xor(j // cpd, lax.axis_index("row"))
    pick = one_hot((m * span + w) * cpd + j % cpd, tokens)
    half = len(order) - len(slots)
    copies = []
    for a in range(0, each // cpd, span):
        parts = []
        for m in range(len(order)):
            i = order.index(m)
            at, ref = (i * each, first) if i < half else (0, slots[i - half])
            parts.append(ref[at + a * cpd : at + (a + span) * cpd, :])
        held[a * cols : (a + span) * cols, :] = dot(pick, jnp.concatenate(parts, 0)).astype(BF)
        rows = pl.ds(a * cols, span * cols)
        copies.append(pltpu.make_async_copy(held.at[rows], out.at[rows], sems.at[len(copies)]))
        copies[-1].start()
    for copy in copies:
        copy.wait()


def final_stage(g, order, first, slots):
    width = first.shape[1]
    tokens = first.shape[0] + sum(a.shape[0] for a in slots)
    return pl.pallas_call(
        functools.partial(final_kernel, g, order),
        in_specs=[VMEM_SPEC] * (1 + len(slots)),
        out_specs=HBM_SPEC,
        out_shape=pltpu.HBM((tokens, width), BF),
        scratch_shapes=[
            pltpu.VMEM((tokens, width), BF),
            pltpu.SemaphoreType.DMA((tokens // (g["span"] * g["cols"]),)),
        ],
        compiler_params=pltpu.CompilerParams(vmem_limit_bytes=8 << 20),
        cost_estimate=pl.CostEstimate(flops=0, bytes_accessed=4 * tokens * width, transcendentals=0),
        name="final_stage",
    )(*[near(a) for a in [first, *slots]])


def swap(x, axis, size, k):
    return x if k == 0 else lax.ppermute(x, axis, [(i, i ^ k) for i in range(size)])


def exchange(parts, axis, order, shift=0):
    n = len(parts)
    size = n << shift
    got = {0: parts[0]}
    for k in order:
        got[k] = swap(parts[k], axis, size, k << shift)
    return [got[k] for k in range(n)]


def deal_kernel(plan, *refs):
    ins, outs = refs[: -len(plan)], refs[-len(plan) :]
    for out, pieces in zip(outs, plan):
        at = 0
        for i, start, size in pieces:
            out[at : at + size, :] = ins[i][start : start + size, :]
            at += size


def deal(ins, plan):
    width = ins[0].shape[1]
    return call(functools.partial(deal_kernel, plan), ins, [(sum(p[2] for p in pieces), width) for pieces in plan], [], 0, far=True)


def row_hop(ins, own, sent, cells, nr):
    came = swap(sent, "row", nr, 1)
    chips = nr // 2
    count = len(ins)
    plan = [own(q) + [(count, start, size) for start, size in cells(q)] for q in range(chips)]
    parts = deal([*ins, came], plan)
    return spread(parts, chip_order(nr))


def spread(parts, order):
    n = len(parts)
    got = {0: parts[0]}
    for q in order:
        got[q] = lax.ppermute(parts[q], "row", [(i, i ^ (2 * q)) for i in range(2 * n)])
    return [got[q] for q in range(n)]


def on_device(nr, nc, latents, row_qkv, row_out, col_qkv, col_out, up_weight, down_weight):
    local_rows, cols, width = latents.shape
    band = local_rows // nc
    rows = band // CHUNKS
    cpd = cols // nr
    chips = nr // 2
    cell = rows * cpd
    g = dict(nr=nr, nc=nc, rows=rows, cols=cols, cpd=cpd, span=8)
    z_order = col_order(nc)

    def enter(t, latents):
        slots = split(latents, nc, band, t * rows, rows)
        slots = [a.reshape(rows * cols, width) for a in slots]
        return exchange(slots, "col", z_order)

    first = enter(0, latents)
    weights = fetch([row_qkv, row_out])
    latents, row_qkv, row_out = lax.optimization_barrier((latents, *weights))
    second = enter(1, latents)

    parts = row_stage(g, nc, first, row_qkv, row_out)
    parts = exchange(parts, "col", z_order)
    half = chips * cell
    (sent,) = deal(parts, [[(k, half, half) for k in range(nc)]])
    slots0 = row_hop(
        parts,
        lambda q: [(k, q * cell, cell) for k in range(nc)],
        sent,
        lambda q: [(k * half + q * cell, cell) for k in range(nc)],
        nr,
    )

    (parts,) = row_stage(g, 1, second, row_qkv, row_out)
    parts = parts.reshape(nr * nc, cell, width)
    parts = lax.all_to_all(parts, ("row", "col"), split_axis=0, concat_axis=0, tiled=True)
    slots1 = parts.reshape(nr * nc * cell, width)

    came = {}
    near_half, far_half = groups(nr)
    for b, members in enumerate((near_half, far_half)):
        if b == 0:
            ins = [slots0, [slots1]]
            old, weights, outs = finish_stage(g, members, ins, col_qkv, col_out, up_weight, down_weight)
        else:
            outs = group_stage(g, members, old, *weights)
        for m, out in zip(members, outs):
            came[m] = swap(out, "row", nr, m)
    done = ffn_stage([came[m] for m in near_half], *weights[1:])
    out = final_stage(g, near_half + far_half, done, [came[m] for m in far_half])
    return out.reshape(local_rows, cols, width)


def col_order(nc):
    return sorted(range(1, nc), key=lambda k: (bin(k).count("1"), -k))


def chip_order(nr):
    return sorted(range(1, nr // 2), key=lambda q: bin(q).count("1"))


def groups(nr):
    near = sorted([*range(2, nr, 2), nr - 1], key=lambda m: (-bin(m // 2).count("1"), m))
    return near, [m for m in range(nr - 1, -1, -1) if m not in near]


def solution(mesh):
    in_specs = (P("row", "col", None), P(), P(), P(), P(), P(), P())
    return jax.shard_map(
        functools.partial(on_device, mesh.shape["row"], mesh.shape["col"]),
        mesh=mesh,
        in_specs=in_specs,
        out_specs=P("row", "col", None),
        check_vma=False,
    )
```
